128 devices in a mesh: tm: 16 (over y, x), rows: 8 (over z, core).
Axes of the slice: x: 4, y: 4, z: 4, core: 2. Of those that a mesh axis runs over, the one named last changes fastest.
Arguments:
- observations: float32 [128, 1024], P('tm'), may hold values from -6 to 6
- observed: int32 [128], P('tm'), may hold values 0 or 1
- start_mean: float32 [1024], replicated, may hold values from -6 to 6
- transition: float32 [1024, 1024], P(('tm', 'rows')), may hold values from -1 to 1
- closed_loop: float32 [1024, 1024], P(('tm', 'rows')), may hold values from -1 to 1
- obs_gain: float32 [1024, 1024], replicated, may hold values from -0.0625 to 0.0625
- smooth_observed: float32 [1024, 1024], P(('tm', 'rows')), may hold values from -1 to 1
- smooth_missing: float32 [1024, 1024], P(('tm', 'rows')), may hold values from -1 to 1
Outputs:
- filtered: float32 [128, 1024], P('tm', 'rows')
- smoothed: float32 [128, 1024], P('tm', 'rows')
The draws below stay inside these ranges and needn't reach their ends.
All inputs are finite; a program needn't handle non-finite values. No bound on the sum of `observed` on one device may be relied on, other than what follows from the above.
Results may differ from the reference program's by a relative error of at most 0.0003.
Values sent between devices are 32-bit elements; how exact they have to be, the bound alone decides.
No kernel may reach another device: no remote copies, remote signals or barrier semaphores. Data moves between devices by JAX's collectives and lax.ppermute only.
A program may use at most 128 MiB of HBM per device.

```python
import math
from functools import partial
import jax
import jax.numpy as jnp
from jax import lax

D = 1024
TIME = 128


precise_dot = partial(jnp.dot, precision=lax.Precision.HIGHEST)


def model_rates(key):
    subkeys = jax.random.split(jax.random.fold_in(key, 7041), 10)
    slow_mask = jax.random.randint(subkeys[0], (D,), 0, 16) < 8
    floor_keep = 0.2
    ceiling_keep = 0.6
    chain_keep = jax.random.uniform(subkeys[2], (D,), jnp.float32, floor_keep, ceiling_keep)
    decay_rate = jnp.where(slow_mask, chain_keep ** (1.0 / TIME), jax.random.uniform(subkeys[3], (D,), jnp.float32, 0.3, 0.85))
    seen_keep = jax.random.uniform(subkeys[4], (D,), jnp.float32, 0.4, 0.8)
    shrink_rate = jnp.where(slow_mask, seen_keep ** (8.0 / TIME), jax.random.uniform(subkeys[5], (D,), jnp.float32, 0.3, 0.7))
    back_keep = jax.random.uniform(subkeys[6], (D,), jnp.float32, floor_keep, ceiling_keep)
    keep_missing = jnp.where(slow_mask, back_keep ** (1.0 / TIME), jax.random.uniform(subkeys[7], (D,), jnp.float32, 0.2, 0.7))
    back_seen = jax.random.uniform(subkeys[8], (D,), jnp.float32, 0.4, 0.8)
    keep_seen = keep_missing * jnp.where(slow_mask, back_seen ** (8.0 / TIME), jax.random.uniform(subkeys[9], (D,), jnp.float32, 0.3, 0.7))
    return (slow_mask, decay_rate, shrink_rate, keep_missing, keep_seen)


def near_orthogonal(key, which_matrix, slow_mask):
    jitter_key = jax.random.fold_in(jax.random.fold_in(key, 5519), which_matrix)
    same_group = (slow_mask[:, None] == slow_mask[None, :]).astype(jnp.float32)
    spread = 0.06 + 0.2 * same_group
    jitter = jax.random.normal(jitter_key, (D, D), jnp.float32) * spread * (1.0 / math.sqrt(D / 2))
    factor = (jnp.eye(D, dtype=jnp.float32) + jitter) / 1.2
    for repeat in range(12):
        factor = 1.5 * factor - 0.5 * precise_dot(precise_dot(factor, factor.T), factor)
    return factor


def draw_transition(key, part):
    slow_mask, decay_rate, shrink_rate, keep_missing, keep_seen = model_rates(key)
    return decay_rate[:, None] * near_orthogonal(key, 11, slow_mask)


def draw_closed_loop(key, part):
    slow_mask, decay_rate, shrink_rate, keep_missing, keep_seen = model_rates(key)
    return (decay_rate * shrink_rate)[:, None] * near_orthogonal(key, 23, slow_mask)


def draw_smooth_observed(key, part):
    slow_mask, decay_rate, shrink_rate, keep_missing, keep_seen = model_rates(key)
    return keep_seen[:, None] * near_orthogonal(key, 37, slow_mask)


def draw_smooth_missing(key, part):
    slow_mask, decay_rate, shrink_rate, keep_missing, keep_seen = model_rates(key)
    return keep_missing[:, None] * near_orthogonal(key, 53, slow_mask)


def place_ends(entries, key, smallest, largest):
    index_at = [jax.random.randint(jax.random.fold_in(key, axis), (), 0, length) for axis, length in enumerate(entries.shape)]
    main_axis = entries.shape.index(max(entries.shape))
    neighbour = index_at[:main_axis] + [(index_at[main_axis] + 1) % entries.shape[main_axis]] + index_at[main_axis + 1:]
    return entries.at[tuple(index_at)].set(smallest).at[tuple(neighbour)].set(largest)


def block_scale(stream_key, shape, cuts, smallest, high):
    gain, own = 1.0, jax.random.fold_in(stream_key, 6)
    for dim, shards_of in cuts:
        steps = jnp.exp(jax.random.uniform(jax.random.fold_in(own, dim), (shards_of,), jnp.float32, smallest / len(cuts), high / len(cuts)))
        gain = gain * jnp.repeat(steps, shape[dim] // shards_of).reshape([-1 if axis == dim else 1 for axis in range(len(shape))])
    return gain


def centred(rng, extent, width, limit, pieces=(), held_as=jnp.bfloat16):
    factor_of = block_scale(rng, extent, pieces, -0.22, 0.18) if pieces else 1.0
    array = jax.random.normal(rng, extent, jnp.float32) * width * factor_of
    return jnp.minimum(jnp.maximum(array, -limit), limit).astype(held_as)


def setup_inputs(seed: int = 0) -> dict:
    key_list = jax.random.split(jax.random.key(seed), 9)
    observations = centred(key_list[0], (TIME, D), 1.0, 6.0, ((0, 16),), jnp.float32)
    observed = place_ends((jax.random.randint(key_list[1], (TIME,), 0, 8) < 1).astype(jnp.int32), jax.random.fold_in(key_list[1], 1), 0, 1)
    start_mean = centred(key_list[2], (D,), 1.0, 6.0, (), jnp.float32)
    transition = draw_transition(jax.random.fold_in(key_list[8], 71), 0)
    closed_loop = draw_closed_loop(jax.random.fold_in(key_list[8], 71), 0)
    obs_gain = centred(key_list[5], (D, D), (8 * D) ** -0.5, 0.0625, (), jnp.float32)
    smooth_observed = draw_smooth_observed(jax.random.fold_in(key_list[8], 71), 0)
    smooth_missing = draw_smooth_missing(jax.random.fold_in(key_list[8], 71), 0)
    return dict(observations=observations, observed=observed, start_mean=start_mean, transition=transition, closed_loop=closed_loop, obs_gain=obs_gain, smooth_observed=smooth_observed, smooth_missing=smooth_missing)


precise_dot = partial(jnp.dot, precision=lax.Precision.HIGHEST)


def reference(observations, observed, start_mean, transition, closed_loop, obs_gain, smooth_observed, smooth_missing):
    seen_float = observed.astype(jnp.float32)
    inject = precise_dot(observations, obs_gain.T) * seen_float[:, None]

    def forward_step(state_vec, inputs):
        is_seen, inject_row = inputs
        matrix = jnp.where(is_seen == 1, closed_loop, transition)
        state_vec = precise_dot(matrix, state_vec) + inject_row
        return state_vec, state_vec

    filtered = lax.scan(forward_step, start_mean, (observed, inject))[1]
    predicted = precise_dot(filtered, transition.T)

    def backward_step(state_vec, inputs):
        is_seen, mean_row, predicted_row = inputs
        matrix = jnp.where(is_seen == 1, smooth_observed, smooth_missing)
        state_vec = mean_row + precise_dot(matrix, state_vec - predicted_row)
        return state_vec, state_vec

    final_mean = filtered[-1]
    earlier = lax.scan(backward_step, final_mean, (observed[:-1], filtered[:-1], predicted[:-1]), reverse=True)[1]
    smoothed = jnp.concatenate([earlier, final_mean[None, :]], 0)
    return filtered, smoothed
```

```python
from functools import partial

import jax
import jax.numpy as jnp
from jax import lax
from jax.experimental import pallas as pl
from jax.experimental.pallas import tpu as pltpu
from jax.sharding import PartitionSpec as P

ALL = ("tm", "rows")
SIDE = 4
CORES = 2
LANES = 128
SUB = 8
UNROLL = 128


def device_id(y, x, z, c):
    return ((y % SIDE * SIDE + x % SIDE) * SIDE + z % SIDE) * CORES + c


def coords():
    return [(y, x, z, c) for y in range(SIDE) for x in range(SIDE) for z in range(SIDE) for c in range(CORES)]


def swap_cores(value):
    return lax.ppermute(value, ALL, [(device_id(y, x, z, c), device_id(y, x, z, 1 - c)) for y, x, z, c in coords()])


def along_z(value, k):
    return lax.ppermute(value, ALL, [(device_id(y, x, z, c), device_id(y, x, z + k, c)) for y, x, z, c in coords()])


def across(value, k, phase):
    pairs = []
    for y, x, z, c in coords():
        dx = k if (c == 0) == (phase == 0) else 0
        dy = k - dx
        pairs.append((device_id(y, x, z, c), device_id(y + dy, x + dx, z, c)))
    return lax.ppermute(value, ALL, pairs)


def tiles(rows):
    r, width = rows.shape
    n = width // LANES
    return rows.reshape(r // SUB, SUB, n, LANES).transpose(0, 2, 1, 3).reshape(r // SUB * n, SUB, LANES)


def load_matrices(place, own, par, mats, sem, blocks):
    y, x, z, c = place[0], place[1], place[2], place[3]

    def start(i, carry):
        k2 = i // SIDE
        kz = i % SIDE
        pz = (z - kz + SIDE) % SIDE
        for k3 in range(SIDE):
            for mine in (True, False):
                q = c if mine else 1 - c
                dy = jnp.where(q == 0, k3, k2)
                dx = jnp.where(q == 0, k2, k3)
                chip = ((y - dy + SIDE) % SIDE * SIDE + (x - dx + SIDE) % SIDE) * SIDE + pz
                src = (own if mine else par)[k3]
                pltpu.make_async_copy(
                    src.at[k2, pl.ds(kz * blocks, blocks)], mats.at[q, pl.ds(chip * blocks, blocks)], sem
                ).start()
        return carry

    lax.fori_loop(0, SIDE * SIDE, start, 0)


def load_inject(place, own, par, inject, sem, first, count):
    y, x, c = place[0], place[1], place[3]

    def start(k2, carry):
        for k3 in range(SIDE):
            for mine in (True, False):
                q = c if mine else 1 - c
                dy = jnp.where(q == 0, k3, k2)
                dx = jnp.where(q == 0, k2, k3)
                seg = (y - dy + SIDE) % SIDE * SIDE + (x - dx + SIDE) % SIDE
                src = (own if mine else par)[k3]
                pltpu.make_async_copy(
                    src.at[k2, pl.ds(first, count)], inject.at[pl.ds(seg * 2 * count + q * count, count)], sem
                ).start()
        return carry

    lax.fori_loop(0, SIDE, start, 0)


def transpose_matrices(mats, mats_t, groups):
    def block(i, carry):
        s = i // (groups * groups)
        b = i // groups % groups
        k = i % groups
        rows = [mats[s, (b * 16 + r) * groups + k] for r in range(16)]
        flipped = jnp.concatenate(rows, 0).T
        for r in range(16):
            mats_t[s, (k * 16 + r) * groups + b] = flipped[r * SUB : (r + 1) * SUB]
        return carry

    lax.fori_loop(0, 2 * groups * groups, block, 0)


def run_chain(place, seen, mats, mats_t, inject, inject_t, start, out, out_t, reverse):
    y, x, c = place[0], place[1], place[3]
    steps, dim = out.shape
    groups = dim // LANES
    row_blocks = dim // SUB
    lane = lax.broadcasted_iota(jnp.int32, (SUB, LANES), 1)

    def pick(t):
        seg = t // SUB
        ky = (y - seg // SIDE + SIDE) % SIDE
        kx = (x - seg % SIDE + SIDE) % SIDE
        k3 = jnp.where(c == 0, ky, kx)
        k2 = jnp.where(c == 0, kx, ky)
        return seen[(k3 * SIDE + k2) * SUB + t % SUB]

    def pair(p, state):
        first = steps - 1 - 2 * p if reverse else 2 * p
        second = first - 1 if reverse else first + 1
        s0, s1 = pick(first), pick(second)
        here = lane == first

        def rows(j, sums):
            r = pl.multiple_of(j * SUB, SUB)
            a = mats[s0, pl.ds(j * groups, groups)]
            prods = [a[k] * state[k] for k in range(groups)]
            while len(prods) > 1:
                prods = [prods[i] + prods[i + 1] for i in range(0, len(prods), 2)]
            total = prods[0] + jnp.where(here, inject_t[pl.ds(r, SUB), :], 0.0)
            col = jnp.broadcast_to(jnp.sum(total, 1, keepdims=True), (SUB, LANES))
            pltpu.store(out_t.at[pl.ds(r, SUB), :], col, mask=here)
            b = mats_t[s1, pl.ds(j * groups, groups)]
            return tuple(sums[k] + b[k] * col for k in range(groups))

        zero = tuple(jnp.zeros((SUB, LANES), jnp.float32) for _ in range(groups))
        sums = lax.fori_loop(0, row_blocks, rows, zero, unroll=UNROLL)
        row = jnp.concatenate([jnp.sum(v, 0, keepdims=True) for v in sums], 1) + inject[pl.ds(second, 1), :]
        out[pl.ds(second, 1), :] = row
        return tuple(jnp.broadcast_to(row[:, k * LANES : (k + 1) * LANES], (SUB, LANES)) for k in range(groups))

    lax.fori_loop(0, steps // 2, pair, start)
    odd = lax.broadcasted_iota(jnp.int32, (steps, LANES), 0) % 2
    from_t = odd == (1 if reverse else 0)
    for k in range(groups):
        cols = slice(k * LANES, (k + 1) * LANES)
        out[:, cols] = jnp.where(from_t, out_t[cols, :].T, out[:, cols])


def split(value):
    high = value.astype(jnp.bfloat16)
    return high, (value - high.astype(jnp.float32)).astype(jnp.bfloat16)


def predict(states, mats_t, out, groups):
    high, low = split(states[...])
    dot = partial(jnp.dot, preferred_element_type=jnp.float32)
    width = 2
    for b in range(0, groups, width):
        weights = jnp.concatenate(
            [
                jnp.concatenate([mats_t[0, j * groups + b + i] for j in range(groups * 16)], 0)
                for i in range(width)
            ],
            1,
        )
        w_high, w_low = split(weights)
        out[:, b * LANES : (b + width) * LANES] = dot(high, w_high) + (dot(low, w_high) + dot(high, w_low))


def forward_kernel(place, seen, start, *refs, groups):
    own, par = refs[:SIDE], refs[SIDE : 2 * SIDE]
    filtered, error, prior, mats, mats_t, inject_tiles, inject, inject_t, out_t, sems = refs[2 * SIDE :]
    dim = filtered.shape[1]
    blocks = 2 * groups
    half = groups // 2
    load_matrices(place, own, par, mats, sems.at[0], blocks)
    load_inject(place, own, par, inject_tiles, sems.at[1], SIDE * blocks, half)
    pltpu.make_async_copy(inject_tiles, inject_tiles, sems.at[1]).wait()
    for seg in range(inject_tiles.shape[0] // groups):
        for k in range(groups):
            inject[seg * SUB : (seg + 1) * SUB, k * LANES : (k + 1) * LANES] = inject_tiles[seg * groups + k]
    for k in range(groups):
        cols = slice(k * LANES, (k + 1) * LANES)
        inject_t[cols, :] = inject[:, cols].T
    pltpu.make_async_copy(mats, mats, sems.at[0]).wait()
    transpose_matrices(mats, mats_t, groups)
    first = tuple(jnp.broadcast_to(start[:, k * LANES : (k + 1) * LANES], (SUB, LANES)) for k in range(groups))
    run_chain(place, seen, mats, mats_t, inject, inject_t, first, filtered, out_t, False)
    predict(filtered, mats_t, inject, groups)
    row = lax.broadcasted_iota(jnp.int32, (filtered.shape[0], LANES), 0)
    for k in range(groups):
        cols = slice(k * LANES, (k + 1) * LANES)
        shifted = jnp.where(row == 0, 0.0, pltpu.roll(inject[:, cols], 1, 0))
        prior[:, cols] = shifted
        error[:, cols] = filtered[:, cols] - shifted


def backward_kernel(place, seen, error, prior, *refs, groups):
    own, par = refs[:SIDE], refs[SIDE : 2 * SIDE]
    smoothed, mats, mats_t, inject_t, out_t, sems = refs[2 * SIDE :]
    blocks = 2 * groups
    load_matrices(place, own, par, mats, sems.at[0], blocks)
    for k in range(groups):
        cols = slice(k * LANES, (k + 1) * LANES)
        inject_t[cols, :] = error[:, cols].T
    pltpu.make_async_copy(mats, mats, sems.at[0]).wait()
    transpose_matrices(mats, mats_t, groups)
    first = tuple(jnp.zeros((SUB, LANES), jnp.float32) for _ in range(groups))
    run_chain(place, seen, mats, mats_t, error, inject_t, first, smoothed, out_t, True)
    smoothed[...] += prior[...]


def shards(observations, observed, start_mean, transition, closed_loop, obs_gain, smooth_observed, smooth_missing):
    seg_steps, dim = observations.shape
    groups = dim // LANES
    steps = seg_steps * lax.axis_size("tm")
    tm = lax.axis_index("tm")
    rows = lax.axis_index("rows")
    y, x, z, c = tm // SIDE, tm % SIDE, rows // CORES, rows % CORES
    place = jnp.stack([y, x, z, c]).astype(jnp.int32)
    is_zero = c == 0

    fwd_0, fwd_1 = tiles(transition), tiles(closed_loop)
    bwd_0, bwd_1 = tiles(smooth_missing), tiles(smooth_observed)
    set_0 = jnp.stack([fwd_0, bwd_0])
    set_1 = jnp.stack([fwd_1, bwd_1])
    mine = jnp.where(is_zero, set_0, set_1)
    other = swap_cores(jnp.where(is_zero, set_1, set_0))
    unit = jnp.where(is_zero, jnp.concatenate([mine, other], 1), jnp.concatenate([other, mine], 1))

    level = [unit] + [along_z(unit, k) for k in range(1, SIDE)]
    gain_rows = lax.dynamic_slice_in_dim(obs_gain, c * (dim // 2), dim // 2, 0)
    seen_float = observed.astype(jnp.float32)
    inject = (
        lax.dot_general(observations, gain_rows, (((1,), (1,)), ((), ())), precision=lax.Precision.HIGHEST)
        * seen_float[:, None]
    )
    seen_tile = jnp.broadcast_to(seen_float[:, None], (seg_steps, LANES))[None]
    packed = jnp.concatenate([u[0] for u in level] + [tiles(inject), seen_tile] + [u[1] for u in level], 0)
    cut = SIDE * 2 * groups + groups // 2 + 1

    packs = [packed] + [across(packed, k, 0) for k in range(1, SIDE)]
    fwd = jnp.stack([p[:cut] for p in packs])
    bwd = jnp.stack([p[cut:] for p in packs])
    fwd_own = [fwd] + [across(fwd, k, 1) for k in range(1, SIDE)]
    fwd_par = [swap_cores(v) for v in fwd_own]
    bwd, fwd_own[1], fwd_own[2], fwd_own[3] = lax.optimization_barrier((bwd, fwd_own[1], fwd_own[2], fwd_own[3]))
    bwd_own = [bwd] + [across(bwd, k, 1) for k in range(1, SIDE)]
    seen = jnp.stack([v[:, cut - 1, :, 0] for v in fwd_own]).astype(jnp.int32).reshape(-1)

    smem = pl.BlockSpec(memory_space=pltpu.SMEM)
    vmem = pl.BlockSpec(memory_space=pltpu.VMEM)
    any_space = pl.BlockSpec(memory_space=pl.ANY)
    full = jax.ShapeDtypeStruct((steps, dim), jnp.float32)
    mats = pltpu.VMEM((2, dim // SUB * groups, SUB, LANES), jnp.float32)
    wide = pltpu.VMEM((steps, dim), jnp.float32)
    tall = pltpu.VMEM((dim, steps), jnp.float32)
    filtered, error, prior = pl.pallas_call(
        partial(forward_kernel, groups=groups),
        out_shape=(full, full, full),
        in_specs=[smem, smem, vmem] + [any_space] * (2 * SIDE),
        out_specs=(vmem, vmem, vmem),
        scratch_shapes=[
            mats,
            mats,
            pltpu.VMEM((steps // SUB * groups, SUB, LANES), jnp.float32),
            wide,
            tall,
            tall,
            pltpu.SemaphoreType.DMA((2,)),
        ],
        name="forward_chain",
    )(place, seen, start_mean.reshape(1, dim), *fwd_own, *fwd_par)

    bwd_par = [swap_cores(v) for v in bwd_own]
    smoothed = pl.pallas_call(
        partial(backward_kernel, groups=groups),
        out_shape=full,
        in_specs=[smem, smem, vmem, vmem] + [any_space] * (2 * SIDE),
        out_specs=vmem,
        scratch_shapes=[mats, mats, tall, tall, pltpu.SemaphoreType.DMA((2,))],
        name="backward_chain",
    )(place, seen, error, prior, *bwd_own, *bwd_par)

    def block(value):
        return lax.dynamic_slice(value, (tm * seg_steps, rows * LANES), (seg_steps, LANES))

    return block(filtered), block(smoothed)


def solution(mesh):
    return jax.shard_map(
        shards,
        mesh=mesh,
        in_specs=(
            P("tm", None),
            P("tm"),
            P(),
            P(("tm", "rows"), None),
            P(("tm", "rows"), None),
            P(),
            P(("tm", "rows"), None),
            P(("tm", "rows"), None),
        ),
        out_specs=(P("tm", "rows"), P("tm", "rows")),
        check_vma=False,
    )
```

```python
from functools import partial

import jax
import jax.numpy as jnp
from jax import lax
from jax.experimental import pallas as pl
from jax.experimental.pallas import tpu as pltpu
from jax.sharding import PartitionSpec as P

ALL = ("tm", "rows")
SIDE = 4
CORES = 2
LANES = 128
SUB = 8
UNROLL = 128
VMEM_BYTES = 28 << 20


def device_id(y, x, z, c):
    return ((y % SIDE * SIDE + x % SIDE) * SIDE + z % SIDE) * CORES + c


def coords():
    return [(y, x, z, c) for y in range(SIDE) for x in range(SIDE) for z in range(SIDE) for c in range(CORES)]


def swap_cores(value):
    return lax.ppermute(value, ALL, [(device_id(y, x, z, c), device_id(y, x, z, 1 - c)) for y, x, z, c in coords()])


def along_z(value, k):
    return lax.ppermute(value, ALL, [(device_id(y, x, z, c), device_id(y, x, z + k, c)) for y, x, z, c in coords()])


def across(value, k, phase):
    pairs = []
    for y, x, z, c in coords():
        dx = k if (c == 0) == (phase == 0) else 0
        dy = k - dx
        pairs.append((device_id(y, x, z, c), device_id(y + dy, x + dx, z, c)))
    return lax.ppermute(value, ALL, pairs)


def tiles(rows):
    r, width = rows.shape
    n = width // LANES
    return rows.reshape(r // SUB, SUB, n, LANES).transpose(0, 2, 1, 3).reshape(r // SUB * n, SUB, LANES)


def whereabouts():
    tm = lax.axis_index("tm")
    rows = lax.axis_index("rows")
    return tm // SIDE, tm % SIDE, rows // CORES, rows % CORES


def load_matrices(place, own, par, mats, blocks):
    y, x, z, c = place

    def move(i, carry):
        k2 = i // SIDE
        kz = i % SIDE
        pz = (z - kz + SIDE) % SIDE
        for k3 in range(SIDE):
            for mine in (True, False):
                q = c if mine else 1 - c
                dy = jnp.where(q == 0, k3, k2)
                dx = jnp.where(q == 0, k2, k3)
                chip = ((y - dy + SIDE) % SIDE * SIDE + (x - dx + SIDE) % SIDE) * SIDE + pz
                src = (own if mine else par)[k3]
                mats[q, pl.ds(chip * blocks, blocks)] = src[k2, pl.ds(kz * blocks, blocks)]
        return carry

    lax.fori_loop(0, SIDE * SIDE, move, 0)


def load_inject(place, own, par, inject, first, count):
    y, x, _, c = place

    def move(k2, carry):
        for k3 in range(SIDE):
            for mine in (True, False):
                q = c if mine else 1 - c
                dy = jnp.where(q == 0, k3, k2)
                dx = jnp.where(q == 0, k2, k3)
                seg = (y - dy + SIDE) % SIDE * SIDE + (x - dx + SIDE) % SIDE
                src = (own if mine else par)[k3]
                inject[pl.ds(seg * 2 * count + q * count, count)] = src[k2, first : first + count]
        return carry

    lax.fori_loop(0, SIDE, move, 0)


def load_seen(place, own, seen, sem, first):
    y, x, _, c = place
    for k3 in range(SIDE):
        for k2 in range(SIDE):
            dy = jnp.where(c == 0, k3, k2)
            dx = jnp.where(c == 0, k2, k3)
            seg = (y - dy + SIDE) % SIDE * SIDE + (x - dx + SIDE) % SIDE
            pltpu.make_async_copy(own[k3].at[k2, first], seen.at[seg], sem).start()


def transpose_matrices(mats, mats_t, groups):
    def block(i, carry):
        s = i // (groups * groups)
        b = i // groups % groups
        k = i % groups
        rows = [mats[s, (b * 16 + r) * groups + k] for r in range(16)]
        flipped = jnp.concatenate(rows, 0).T
        for r in range(16):
            mats_t[s, (k * 16 + r) * groups + b] = flipped[r * SUB : (r + 1) * SUB]
        return carry

    lax.fori_loop(0, 2 * groups * groups, block, 0, unroll=16)


def run_chain(seen, mats, mats_t, inject, inject_t, start, out, out_t, reverse):
    steps, dim = out.shape
    groups = dim // LANES
    row_blocks = dim // SUB
    lane = lax.broadcasted_iota(jnp.int32, (SUB, LANES), 1)

    def pick(t):
        return (seen[t // SUB, t % SUB, 0] > 0.5).astype(jnp.int32)

    def pair(p, state):
        first = steps - 1 - 2 * p if reverse else 2 * p
        second = first - 1 if reverse else first + 1
        s0, s1 = pick(first), pick(second)
        here = lane == first

        def rows(j, sums):
            r = pl.multiple_of(j * SUB, SUB)
            a = mats[s0, pl.ds(j * groups, groups)]
            prods = [a[k] * state[k] for k in range(groups)]
            while len(prods) > 1:
                prods = [prods[i] + prods[i + 1] for i in range(0, len(prods), 2)]
            total = prods[0] + jnp.where(here, inject_t[pl.ds(r, SUB), :], 0.0)
            col = jnp.broadcast_to(jnp.sum(total, 1, keepdims=True), (SUB, LANES))
            pltpu.store(out_t.at[pl.ds(r, SUB), :], col, mask=here)
            b = mats_t[s1, pl.ds(j * groups, groups)]
            return tuple(sums[k] + b[k] * col for k in range(groups))

        zero = tuple(jnp.zeros((SUB, LANES), jnp.float32) for _ in range(groups))
        sums = lax.fori_loop(0, row_blocks, rows, zero, unroll=UNROLL)
        row = jnp.concatenate([jnp.sum(v, 0, keepdims=True) for v in sums], 1) + inject[pl.ds(second, 1), :]
        out[pl.ds(second, 1), :] = row
        return tuple(jnp.broadcast_to(row[:, k * LANES : (k + 1) * LANES], (SUB, LANES)) for k in range(groups))

    lax.fori_loop(0, steps // 2, pair, start)
    odd = lax.broadcasted_iota(jnp.int32, (steps, LANES), 0) % 2
    from_t = odd == (1 if reverse else 0)
    for k in range(groups):
        cols = slice(k * LANES, (k + 1) * LANES)
        out[:, cols] = jnp.where(from_t, out_t[cols, :].T, out[:, cols])


def split(value):
    high = value.astype(jnp.bfloat16)
    return high, (value - high.astype(jnp.float32)).astype(jnp.bfloat16)


def predict(states, mats_t, out, groups):
    high, low = split(states[...])
    dot = partial(jnp.dot, preferred_element_type=jnp.float32)
    width = 2
    for b in range(0, groups, width):
        weights = jnp.concatenate(
            [
                jnp.concatenate([mats_t[0, j * groups + b + i] for j in range(groups * 16)], 0)
                for i in range(width)
            ],
            1,
        )
        w_high, w_low = split(weights)
        out[:, b * LANES : (b + width) * LANES] = dot(high, w_high) + (dot(low, w_high) + dot(high, w_low))


def send_block(place, value, block, sem):
    y, x, z, c = place
    seg_steps, width = block.shape
    corner = pl.ds((y * SIDE + x) * seg_steps, seg_steps), pl.ds((z * CORES + c) * width, width)
    pltpu.make_async_copy(value.at[corner], block, sem).start()


def forward_kernel(start, *refs, groups):
    own, par = refs[:SIDE], refs[SIDE : 2 * SIDE]
    block, error, prior, filtered, seen, mats, mats_t, inject_tiles, inject, inject_t, out_t, sems = refs[2 * SIDE :]
    dim = filtered.shape[1]
    blocks = 2 * groups
    half = groups // 2
    place = whereabouts()
    load_seen(place, own, seen, sems.at[0], SIDE * blocks + half)
    load_matrices(place, own, par, mats, blocks)
    load_inject(place, own, par, inject_tiles, SIDE * blocks, half)
    for seg in range(inject_tiles.shape[0] // groups):
        for k in range(groups):
            inject[seg * SUB : (seg + 1) * SUB, k * LANES : (k + 1) * LANES] = inject_tiles[seg * groups + k]
    for k in range(groups):
        cols = slice(k * LANES, (k + 1) * LANES)
        inject_t[cols, :] = inject[:, cols].T
    transpose_matrices(mats, mats_t, groups)
    first = tuple(jnp.broadcast_to(start[:, k * LANES : (k + 1) * LANES], (SUB, LANES)) for k in range(groups))
    pltpu.make_async_copy(seen, seen, sems.at[0]).wait()
    run_chain(seen, mats, mats_t, inject, inject_t, first, filtered, out_t, False)
    send_block(place, filtered, block, sems.at[1])
    predict(filtered, mats_t, inject, groups)
    row = lax.broadcasted_iota(jnp.int32, (filtered.shape[0], LANES), 0)
    for k in range(groups):
        cols = slice(k * LANES, (k + 1) * LANES)
        shifted = jnp.where(row == 0, 0.0, pltpu.roll(inject[:, cols], 1, 0))
        prior[:, cols] = shifted
        error[:, cols] = filtered[:, cols] - shifted
    pltpu.make_async_copy(filtered.at[: block.shape[0], : block.shape[1]], block, sems.at[1]).wait()


def backward_kernel(error, prior, *refs, groups):
    own, par, fwd = refs[:SIDE], refs[SIDE : 2 * SIDE], refs[2 * SIDE : 3 * SIDE]
    block, smoothed, seen, mats, mats_t, inject_t, out_t, sems = refs[3 * SIDE :]
    blocks = 2 * groups
    place = whereabouts()
    load_seen(place, fwd, seen, sems.at[0], SIDE * blocks + groups // 2)
    load_matrices(place, own, par, mats, blocks)
    for k in range(groups):
        cols = slice(k * LANES, (k + 1) * LANES)
        inject_t[cols, :] = error[:, cols].T
    transpose_matrices(mats, mats_t, groups)
    first = tuple(jnp.zeros((SUB, LANES), jnp.float32) for _ in range(groups))
    pltpu.make_async_copy(seen, seen, sems.at[0]).wait()
    run_chain(seen, mats, mats_t, error, inject_t, first, smoothed, out_t, True)
    smoothed[...] += prior[...]
    send_block(place, smoothed, block, sems.at[1])
    pltpu.make_async_copy(smoothed.at[: block.shape[0], : block.shape[1]], block, sems.at[1]).wait()


def shards(observations, observed, start_mean, transition, closed_loop, obs_gain, smooth_observed, smooth_missing):
    seg_steps, dim = observations.shape
    groups = dim // LANES
    steps = seg_steps * lax.axis_size("tm")
    c = lax.axis_index("rows") % CORES
    is_zero = c == 0

    fwd_0, fwd_1 = tiles(transition), tiles(closed_loop)
    bwd_0, bwd_1 = tiles(smooth_missing), tiles(smooth_observed)
    set_0 = jnp.stack([fwd_0, bwd_0])
    set_1 = jnp.stack([fwd_1, bwd_1])
    mine = jnp.where(is_zero, set_0, set_1)
    other = swap_cores(jnp.where(is_zero, set_1, set_0))
    unit = jnp.where(is_zero, jnp.concatenate([mine, other], 1), jnp.concatenate([other, mine], 1))

    gain_rows = lax.dynamic_slice_in_dim(obs_gain, c * (dim // 2), dim // 2, 0)
    seen_float = observed.astype(jnp.float32)
    inject = (
        lax.dot_general(observations, gain_rows, (((1,), (1,)), ((), ())), precision=lax.Precision.HIGHEST)
        * seen_float[:, None]
    )
    late, inject = lax.optimization_barrier((unit, inject))
    level = [unit, along_z(unit, 1), along_z(unit, 2), along_z(late, 3)]
    seen_tile = jnp.broadcast_to(seen_float[:, None], (seg_steps, LANES))[None]
    packed = jnp.concatenate([u[0] for u in level] + [tiles(inject), seen_tile] + [u[1] for u in level], 0)
    cut = SIDE * 2 * groups + groups // 2 + 1

    packs = [packed] + [across(packed, k, 0) for k in range(1, SIDE)]
    fwd = jnp.stack([p[:cut] for p in packs])
    bwd = jnp.stack([p[cut:] for p in packs])
    fwd_own = [fwd] + [across(fwd, k, 1) for k in range(1, SIDE)]
    fwd_par = [swap_cores(v) for v in fwd_own]
    bwd_own = [bwd] + [across(bwd, k, 1) for k in range(1, SIDE)]
    vmem = pl.BlockSpec(memory_space=pltpu.VMEM)
    any_space = pl.BlockSpec(memory_space=pl.ANY)
    full = jax.ShapeDtypeStruct((steps, dim), jnp.float32)
    mats = pltpu.VMEM((2, dim // SUB * groups, SUB, LANES), jnp.float32)
    wide = pltpu.VMEM((steps, dim), jnp.float32)
    tall = pltpu.VMEM((dim, steps), jnp.float32)
    seen = pltpu.SMEM((steps // SUB, SUB, LANES), jnp.float32)
    out_block = jax.ShapeDtypeStruct((seg_steps, LANES), jnp.float32)
    filtered, error, prior = pl.pallas_call(
        partial(forward_kernel, groups=groups),
        out_shape=(out_block, full, full),
        in_specs=[vmem] * (1 + 2 * SIDE),
        out_specs=(any_space, vmem, vmem),
        scratch_shapes=[
            wide,
            seen,
            mats,
            mats,
            pltpu.VMEM((steps // SUB * groups, SUB, LANES), jnp.float32),
            wide,
            tall,
            tall,
            pltpu.SemaphoreType.DMA((2,)),
        ],
        compiler_params=pltpu.CompilerParams(vmem_limit_bytes=VMEM_BYTES),
        name="forward_chain",
    )(start_mean.reshape(1, dim), *fwd_own, *fwd_par)

    *moved, error = lax.optimization_barrier((*bwd_own[1:], error))
    bwd_own = bwd_own[:1] + moved
    bwd_par = [swap_cores(v) for v in bwd_own]
    smoothed = pl.pallas_call(
        partial(backward_kernel, groups=groups),
        out_shape=out_block,
        in_specs=[vmem] * (2 + 2 * SIDE) + [any_space] * SIDE,
        out_specs=any_space,
        scratch_shapes=[wide, seen, mats, mats, tall, tall, pltpu.SemaphoreType.DMA((2,))],
        compiler_params=pltpu.CompilerParams(vmem_limit_bytes=VMEM_BYTES),
        name="backward_chain",
    )(error, prior, *bwd_own, *bwd_par, *fwd_own)
    return filtered, smoothed


def solution(mesh):
    return jax.shard_map(
        shards,
        mesh=mesh,
        in_specs=(
            P("tm", None),
            P("tm"),
            P(),
            P(("tm", "rows"), None),
            P(("tm", "rows"), None),
            P(),
            P(("tm", "rows"), None),
            P(("tm", "rows"), None),
        ),
        out_specs=(P("tm", "rows"), P("tm", "rows")),
        check_vma=False,
    )
```

```python
from functools import partial

import jax
import jax.numpy as jnp
from jax import lax
from jax.experimental import pallas as pl
from jax.experimental.pallas import tpu as pltpu
from jax.sharding import PartitionSpec as P


ALL = ("tm", "rows")
SIDE = 4
CORES = 2
LANES = 128
SUB = 8
UNROLL = 128
VMEM_BYTES = 28 << 20


def device_id(y, x, z, c):
    return ((y % SIDE * SIDE + x % SIDE) * SIDE + z % SIDE) * CORES + c


def coords():
    return [(y, x, z, c) for y in range(SIDE) for x in range(SIDE) for z in range(SIDE) for c in range(CORES)]


def swap_cores(value):
    return lax.ppermute(value, ALL, [(device_id(y, x, z, c), device_id(y, x, z, 1 - c)) for y, x, z, c in coords()])


def along_z(value, k):
    return lax.ppermute(value, ALL, [(device_id(y, x, z, c), device_id(y, x, z + k, c)) for y, x, z, c in coords()])


def across(value, k, phase):
    pairs = []
    for y, x, z, c in coords():
        dx = k if (c == 0) == (phase == 0) else 0
        dy = k - dx
        pairs.append((device_id(y, x, z, c), device_id(y + dy, x + dx, z, c)))
    return lax.ppermute(value, ALL, pairs)


def tiles(rows):
    r, width = rows.shape
    n = width // LANES
    return rows.reshape(r // SUB, SUB, n, LANES).transpose(0, 2, 1, 3).reshape(r // SUB * n, SUB, LANES)


def whereabouts():
    tm = lax.axis_index("tm")
    rows = lax.axis_index("rows")
    return tm // SIDE, tm % SIDE, rows // CORES, rows % CORES


def load_matrices(place, own, par, mats, blocks):
    y, x, z, c = place

    def move(i, carry):
        k2 = i // SIDE
        kz = i % SIDE
        pz = (z - kz + SIDE) % SIDE
        for k3 in range(SIDE):
            for mine in (True, False):
                q = c if mine else 1 - c
                dy = jnp.where(q == 0, k3, k2)
                dx = jnp.where(q == 0, k2, k3)
                chip = ((y - dy + SIDE) % SIDE * SIDE + (x - dx + SIDE) % SIDE) * SIDE + pz
                src = (own if mine else par)[k3]
                mats[q, pl.ds(chip * blocks, blocks)] = src[k2, pl.ds(kz * blocks, blocks)]
        return carry

    lax.fori_loop(0, SIDE * SIDE, move, 0)


def load_inject(place, own, par, inject, first, count):
    y, x, _, c = place

    def move(k2, carry):
        for k3 in range(SIDE):
            for mine in (True, False):
                q = c if mine else 1 - c
                dy = jnp.where(q == 0, k3, k2)
                dx = jnp.where(q == 0, k2, k3)
                seg = (y - dy + SIDE) % SIDE * SIDE + (x - dx + SIDE) % SIDE
                src = (own if mine else par)[k3]
                inject[pl.ds(seg * 2 * count + q * count, count)] = src[k2, first : first + count]
        return carry

    lax.fori_loop(0, SIDE, move, 0)


def load_seen(place, own, seen, sem, first):
    y, x, _, c = place
    for k3 in range(SIDE):
        for k2 in range(SIDE):
            dy = jnp.where(c == 0, k3, k2)
            dx = jnp.where(c == 0, k2, k3)
            seg = (y - dy + SIDE) % SIDE * SIDE + (x - dx + SIDE) % SIDE
            pltpu.make_async_copy(own[k3].at[k2, first], seen.at[seg], sem).start()


def transpose_matrices(mats, mats_t, groups):
    def block(i, carry):
        s = i // (groups * groups)
        b = i // groups % groups
        k = i % groups
        rows = [mats[s, (b * 16 + r) * groups + k] for r in range(16)]
        flipped = jnp.concatenate(rows, 0).T
        for r in range(16):
            mats_t[s, (k * 16 + r) * groups + b] = flipped[r * SUB : (r + 1) * SUB]
        return carry

    lax.fori_loop(0, 2 * groups * groups, block, 0, unroll=16)


def run_chain(seen, mats, mats_t, inject, inject_t, start, out, out_t, reverse):
    steps, dim = out.shape
    groups = dim // LANES
    row_blocks = dim // SUB
    lane = lax.broadcasted_iota(jnp.int32, (SUB, LANES), 1)

    def pick(t):
        return (seen[t // SUB, t % SUB, 0] > 0.5).astype(jnp.int32)

    def pair(p, state):
        first = steps - 1 - 2 * p if reverse else 2 * p
        second = first - 1 if reverse else first + 1
        s0, s1 = pick(first), pick(second)
        here = lane == first

        def rows(j, sums):
            r = pl.multiple_of(j * SUB, SUB)
            a = mats[s0, pl.ds(j * groups, groups)]
            prods = [a[k] * state[k] for k in range(groups)]
            while len(prods) > 1:
                prods = [prods[i] + prods[i + 1] for i in range(0, len(prods), 2)]
            total = prods[0] + jnp.where(here, inject_t[pl.ds(r, SUB), :], 0.0)
            col = jnp.broadcast_to(jnp.sum(total, 1, keepdims=True), (SUB, LANES))
            pltpu.store(out_t.at[pl.ds(r, SUB), :], col, mask=here)
            b = mats_t[s1, pl.ds(j * groups, groups)]
            return tuple(sums[k] + b[k] * col for k in range(groups))

        zero = tuple(jnp.zeros((SUB, LANES), jnp.float32) for _ in range(groups))
        sums = lax.fori_loop(0, row_blocks, rows, zero, unroll=UNROLL)
        row = jnp.concatenate([jnp.sum(v, 0, keepdims=True) for v in sums], 1) + inject[pl.ds(second, 1), :]
        out[pl.ds(second, 1), :] = row
        return tuple(jnp.broadcast_to(row[:, k * LANES : (k + 1) * LANES], (SUB, LANES)) for k in range(groups))

    lax.fori_loop(0, steps // 2, pair, start)
    odd = lax.broadcasted_iota(jnp.int32, (steps, LANES), 0) % 2
    from_t = odd == (1 if reverse else 0)
    for k in range(groups):
        cols = slice(k * LANES, (k + 1) * LANES)
        out[:, cols] = jnp.where(from_t, out_t[cols, :].T, out[:, cols])


def split(value):
    high = value.astype(jnp.bfloat16)
    return high, (value - high.astype(jnp.float32)).astype(jnp.bfloat16)


def predict(states, mats_t, out, groups):
    high, low = split(states[...])
    dot = partial(jnp.dot, preferred_element_type=jnp.float32)
    width = 2
    for b in range(0, groups, width):
        weights = jnp.concatenate(
            [
                jnp.concatenate([mats_t[0, j * groups + b + i] for j in range(groups * 16)], 0)
                for i in range(width)
            ],
            1,
        )
        w_high, w_low = split(weights)
        out[:, b * LANES : (b + width) * LANES] = dot(high, w_high) + (dot(low, w_high) + dot(high, w_low))


def send_block(place, value, block, sem):
    y, x, z, c = place
    seg_steps, width = block.shape
    corner = pl.ds((y * SIDE + x) * seg_steps, seg_steps), pl.ds((z * CORES + c) * width, width)
    pltpu.make_async_copy(value.at[corner], block, sem).start()


def forward_kernel(start, *refs, groups):
    own, par = refs[:SIDE], refs[SIDE : 2 * SIDE]
    block, error, prior, filtered, seen, mats, mats_t, inject_tiles, inject, inject_t, out_t, sems = refs[2 * SIDE :]
    blocks = 2 * groups
    half = groups // 2
    place = whereabouts()
    load_seen(place, own, seen, sems.at[0], SIDE * blocks + half)
    load_matrices(place, own, par, mats, blocks)
    load_inject(place, own, par, inject_tiles, SIDE * blocks, half)
    for seg in range(inject_tiles.shape[0] // groups):
        for k in range(groups):
            inject[seg * SUB : (seg + 1) * SUB, k * LANES : (k + 1) * LANES] = inject_tiles[seg * groups + k]
    for k in range(groups):
        cols = slice(k * LANES, (k + 1) * LANES)
        inject_t[cols, :] = inject[:, cols].T
    transpose_matrices(mats, mats_t, groups)
    first = tuple(jnp.broadcast_to(start[:, k * LANES : (k + 1) * LANES], (SUB, LANES)) for k in range(groups))
    pltpu.make_async_copy(seen, seen, sems.at[0]).wait()
    run_chain(seen, mats, mats_t, inject, inject_t, first, filtered, out_t, False)
    send_block(place, filtered, block, sems.at[1])
    predict(filtered, mats_t, inject, groups)
    row = lax.broadcasted_iota(jnp.int32, (filtered.shape[0], LANES), 0)
    for k in range(groups):
        cols = slice(k * LANES, (k + 1) * LANES)
        shifted = jnp.where(row == 0, 0.0, pltpu.roll(inject[:, cols], 1, 0))
        prior[:, cols] = shifted
        error[:, cols] = filtered[:, cols] - shifted
    pltpu.make_async_copy(filtered.at[: block.shape[0], : block.shape[1]], block, sems.at[1]).wait()


def backward_kernel(error, prior, *refs, groups):
    own, par, fwd = refs[:SIDE], refs[SIDE : 2 * SIDE], refs[2 * SIDE : 3 * SIDE]
    block, smoothed, seen, mats, mats_t, inject_t, out_t, sems = refs[3 * SIDE :]
    blocks = 2 * groups
    place = whereabouts()
    load_seen(place, fwd, seen, sems.at[0], SIDE * blocks + groups // 2)
    load_matrices(place, own, par, mats, blocks)
    for k in range(groups):
        cols = slice(k * LANES, (k + 1) * LANES)
        inject_t[cols, :] = error[:, cols].T
    transpose_matrices(mats, mats_t, groups)
    first = tuple(jnp.zeros((SUB, LANES), jnp.float32) for _ in range(groups))
    pltpu.make_async_copy(seen, seen, sems.at[0]).wait()
    run_chain(seen, mats, mats_t, error, inject_t, first, smoothed, out_t, True)
    smoothed[...] += prior[...]
    send_block(place, smoothed, block, sems.at[1])
    pltpu.make_async_copy(smoothed.at[: block.shape[0], : block.shape[1]], block, sems.at[1]).wait()


def shards(observations, observed, start_mean, transition, closed_loop, obs_gain, smooth_observed, smooth_missing):
    seg_steps, dim = observations.shape
    groups = dim // LANES
    steps = seg_steps * lax.axis_size("tm")
    c = lax.axis_index("rows") % CORES
    is_zero = c == 0

    fwd_0, fwd_1 = tiles(transition), tiles(closed_loop)
    bwd_0, bwd_1 = tiles(smooth_missing), tiles(smooth_observed)
    set_0 = jnp.stack([fwd_0, bwd_0])
    set_1 = jnp.stack([fwd_1, bwd_1])
    mine = jnp.where(is_zero, set_0, set_1)
    other = swap_cores(jnp.where(is_zero, set_1, set_0))
    unit = jnp.where(is_zero, jnp.concatenate([mine, other], 1), jnp.concatenate([other, mine], 1))

    gain_rows = lax.dynamic_slice_in_dim(obs_gain, c * (dim // 2), dim // 2, 0)
    seen_float = observed.astype(jnp.float32)
    inject = (
        lax.dot_general(observations, gain_rows, (((1,), (1,)), ((), ())), precision=lax.Precision.HIGHEST)
        * seen_float[:, None]
    )
    level = [unit]
    for k in range(1, SIDE):
        level.append(along_z(unit, k))
    inject = lax.optimization_barrier(inject)
    seen_tile = jnp.broadcast_to(seen_float[:, None], (seg_steps, LANES))[None]
    packed = jnp.concatenate([u[0] for u in level] + [tiles(inject), seen_tile] + [u[1] for u in level], 0)
    cut = SIDE * 2 * groups + groups // 2 + 1

    packs = [packed] + [across(packed, k, 0) for k in range(1, SIDE)]
    fwd = jnp.stack([p[:cut] for p in packs])
    bwd = jnp.stack([p[cut:] for p in packs])
    fwd_own = [fwd] + [across(fwd, k, 1) for k in range(1, SIDE)]
    fwd_par = [swap_cores(v) for v in fwd_own]
    bwd_own = [bwd] + [across(bwd, k, 1) for k in range(1, SIDE)]
    vmem = pl.BlockSpec(memory_space=pltpu.VMEM)
    any_space = pl.BlockSpec(memory_space=pl.ANY)
    full = jax.ShapeDtypeStruct((steps, dim), jnp.float32)
    mats = pltpu.VMEM((2, dim // SUB * groups, SUB, LANES), jnp.float32)
    wide = pltpu.VMEM((steps, dim), jnp.float32)
    tall = pltpu.VMEM((dim, steps), jnp.float32)
    seen = pltpu.SMEM((steps // SUB, SUB, LANES), jnp.float32)
    out_block = jax.ShapeDtypeStruct((seg_steps, LANES), jnp.float32)
    filtered, error, prior = pl.pallas_call(
        partial(forward_kernel, groups=groups),
        out_shape=(out_block, full, full),
        in_specs=[vmem] * (1 + 2 * SIDE),
        out_specs=(any_space, vmem, vmem),
        scratch_shapes=[
            wide,
            seen,
            mats,
            mats,
            pltpu.VMEM((steps // SUB * groups, SUB, LANES), jnp.float32),
            wide,
            tall,
            tall,
            pltpu.SemaphoreType.DMA((2,)),
        ],
        compiler_params=pltpu.CompilerParams(vmem_limit_bytes=VMEM_BYTES),
        name="forward_chain",
    )(start_mean.reshape(1, dim), *fwd_own, *fwd_par)

    *moved, error = lax.optimization_barrier((*bwd_own[1:], error))
    bwd_own = bwd_own[:1] + moved
    bwd_par = [swap_cores(v) for v in bwd_own]
    smoothed = pl.pallas_call(
        partial(backward_kernel, groups=groups),
        out_shape=out_block,
        in_specs=[vmem] * (2 + 2 * SIDE) + [any_space] * SIDE,
        out_specs=any_space,
        scratch_shapes=[wide, seen, mats, mats, tall, tall, pltpu.SemaphoreType.DMA((2,))],
        compiler_params=pltpu.CompilerParams(vmem_limit_bytes=VMEM_BYTES),
        name="backward_chain",
    )(error, prior, *bwd_own, *bwd_par, *fwd_own)
    return filtered, smoothed


def solution(mesh):
    return jax.shard_map(
        shards,
        mesh=mesh,
        in_specs=(
            P("tm", None),
            P("tm"),
            P(),
            P(("tm", "rows"), None),
            P(("tm", "rows"), None),
            P(),
            P(("tm", "rows"), None),
            P(("tm", "rows"), None),
        ),
        out_specs=(P("tm", "rows"), P("tm", "rows")),
        check_vma=False,
    )
```

```python
from functools import partial

import jax
import jax.numpy as jnp
from jax import lax
from jax.experimental import pallas as pl
from jax.experimental.pallas import tpu as pltpu
from jax.sharding import PartitionSpec as P


ALL = ("tm", "rows")
SIDE = 4
CORES = 2
LANES = 128
SUB = 8
UNROLL = 128
FIRST_STEPS = 80
VMEM_BYTES = 28 << 20
FIRST_BYTES = 8 << 20


def device_id(y, x, z, c):
    return ((y % SIDE * SIDE + x % SIDE) * SIDE + z % SIDE) * CORES + c


def coords():
    return [(y, x, z, c) for y in range(SIDE) for x in range(SIDE) for z in range(SIDE) for c in range(CORES)]


def swap_cores(value):
    return lax.ppermute(value, ALL, [(device_id(y, x, z, c), device_id(y, x, z, 1 - c)) for y, x, z, c in coords()])


def along_z(value, k):
    return lax.ppermute(value, ALL, [(device_id(y, x, z, c), device_id(y, x, z + k, c)) for y, x, z, c in coords()])


def across(value, k, phase):
    pairs = []
    for y, x, z, c in coords():
        dx = k if (c == 0) == (phase == 0) else 0
        dy = k - dx
        pairs.append((device_id(y, x, z, c), device_id(y + dy, x + dx, z, c)))
    return lax.ppermute(value, ALL, pairs)


def tiles(rows):
    r, width = rows.shape
    n = width // LANES
    return rows.reshape(r // SUB, SUB, n, LANES).transpose(0, 2, 1, 3).reshape(r // SUB * n, SUB, LANES)


def whereabouts():
    tm = lax.axis_index("tm")
    rows = lax.axis_index("rows")
    return tm // SIDE, tm % SIDE, rows // CORES, rows % CORES


def load_matrices(place, own, par, mats, blocks):
    y, x, z, c = place

    def move(i, carry):
        k2 = i // SIDE
        kz = i % SIDE
        pz = (z - kz + SIDE) % SIDE
        for k3 in range(SIDE):
            for mine in (True, False):
                q = c if mine else 1 - c
                dy = jnp.where(q == 0, k3, k2)
                dx = jnp.where(q == 0, k2, k3)
                chip = ((y - dy + SIDE) % SIDE * SIDE + (x - dx + SIDE) % SIDE) * SIDE + pz
                src = (own if mine else par)[k3]
                mats[q, pl.ds(chip * blocks, blocks)] = src[k2, pl.ds(kz * blocks, blocks)]
        return carry

    lax.fori_loop(0, SIDE * SIDE, move, 0)


def load_inject(place, own, par, inject, first, count):
    y, x, _, c = place

    def move(k2, carry):
        for k3 in range(SIDE):
            for mine in (True, False):
                q = c if mine else 1 - c
                dy = jnp.where(q == 0, k3, k2)
                dx = jnp.where(q == 0, k2, k3)
                seg = (y - dy + SIDE) % SIDE * SIDE + (x - dx + SIDE) % SIDE
                src = (own if mine else par)[k3]
                inject[pl.ds(seg * 2 * count + q * count, count)] = src[k2, first : first + count]
        return carry

    lax.fori_loop(0, SIDE, move, 0)


def load_seen(place, own, seen, first):
    y, x, _, c = place
    lane = lax.broadcasted_iota(jnp.int32, (SUB, LANES), 1)
    sub = lax.broadcasted_iota(jnp.int32, (SUB, LANES), 0)
    for k3 in range(SIDE):
        for k2 in range(SIDE):
            dy = jnp.where(c == 0, k3, k2)
            dx = jnp.where(c == 0, k2, k3)
            seg = (y - dy + SIDE) % SIDE * SIDE + (x - dx + SIDE) % SIDE
            flags = jnp.where(lane == sub, own[k3][k2, first], 0.0)
            seen[pl.ds(seg, 1), :] = jnp.sum(flags, 0, keepdims=True)


def transpose_matrices(mats, mats_t, groups):
    def block(i, carry):
        s = i // (groups * groups)
        b = i // groups % groups
        k = i % groups
        rows = [mats[s, (b * 16 + r) * groups + k] for r in range(16)]
        flipped = jnp.concatenate(rows, 0).T
        for r in range(16):
            mats_t[s, (k * 16 + r) * groups + b] = flipped[r * SUB : (r + 1) * SUB]
        return carry

    lax.fori_loop(0, 2 * groups * groups, block, 0, unroll=16)


def run_chain(seen, mats, mats_t, inject, inject_t, start, out, out_t, reverse, begin, count):
    steps, dim = inject.shape
    groups = dim // LANES
    row_blocks = dim // SUB
    lane = lax.broadcasted_iota(jnp.int32, (SUB, LANES), 1)

    def pick(t):
        return (seen[t // SUB, t % SUB] > 0.5).astype(jnp.int32)

    def pair(p, row):
        first = steps - 1 - begin - 2 * p if reverse else begin + 2 * p
        second = first - 1 if reverse else first + 1
        s0, s1 = pick(first), pick(second)
        here = lane == first
        state = [jnp.broadcast_to(row[:, k * LANES : (k + 1) * LANES], (SUB, LANES)) for k in range(groups)]

        def rows(j, sums):
            r = pl.multiple_of(j * SUB, SUB)
            a = mats[s0, pl.ds(j * groups, groups)]
            prods = [a[k] * state[k] for k in range(groups)]
            while len(prods) > 1:
                prods = [prods[i] + prods[i + 1] for i in range(0, len(prods), 2)]
            total = prods[0] + jnp.where(here, inject_t[pl.ds(r, SUB), :], 0.0)
            col = jnp.broadcast_to(jnp.sum(total, 1, keepdims=True), (SUB, LANES))
            pltpu.store(out_t.at[pl.ds(r, SUB), :], col, mask=here)
            b = mats_t[s1, pl.ds(j * groups, groups)]
            return tuple(sums[k] + b[k] * col for k in range(groups))

        zero = tuple(jnp.zeros((SUB, LANES), jnp.float32) for _ in range(groups))
        sums = lax.fori_loop(0, row_blocks, rows, zero, unroll=UNROLL)
        row = jnp.concatenate([jnp.sum(v, 0, keepdims=True) for v in sums], 1) + inject[pl.ds(second, 1), :]
        out[pl.ds(second, 1), :] = row
        return row

    lax.fori_loop(0, count // 2, pair, start)
    low = steps - begin - count if reverse else begin
    odd = lax.broadcasted_iota(jnp.int32, (count, LANES), 0) % 2
    from_t = odd == (1 if reverse else 0)
    for k in range(groups):
        cols = slice(k * LANES, (k + 1) * LANES)
        flipped = out_t[cols, :].T[low : low + count]
        out[low : low + count, cols] = jnp.where(from_t, flipped, out[low : low + count, cols])


def split(value):
    high = value.astype(jnp.bfloat16)
    return high, (value - high.astype(jnp.float32)).astype(jnp.bfloat16)


def predict(states, mats_t, out, groups):
    high, low = split(states[...])
    dot = partial(jnp.dot, preferred_element_type=jnp.float32)
    width = 2
    for b in range(0, groups, width):
        weights = jnp.concatenate(
            [
                jnp.concatenate([mats_t[0, j * groups + b + i] for j in range(groups * 16)], 0)
                for i in range(width)
            ],
            1,
        )
        w_high, w_low = split(weights)
        out[:, b * LANES : (b + width) * LANES] = dot(high, w_high) + (dot(low, w_high) + dot(high, w_low))


def send_block(place, value, block, sem):
    y, x, z, c = place
    seg_steps, width = block.shape
    corner = pl.ds((y * SIDE + x) * seg_steps, seg_steps), pl.ds((z * CORES + c) * width, width)
    pltpu.make_async_copy(value.at[corner], block, sem).start()


def first_kernel(start, *refs, groups):
    own, par = refs[:SIDE], refs[SIDE : 2 * SIDE]
    filtered, mats, mats_t, inject, inject_t, seen, inject_tiles, out_t, seen_now, sem = refs[2 * SIDE :]
    blocks = 2 * groups
    half = groups // 2
    place = whereabouts()
    load_seen(place, own, seen, SIDE * blocks + half)
    copy_seen = pltpu.make_async_copy(seen, seen_now, sem.at[0])
    copy_seen.start()
    load_matrices(place, own, par, mats, blocks)
    load_inject(place, own, par, inject_tiles, SIDE * blocks, half)
    for seg in range(inject_tiles.shape[0] // groups):
        for k in range(groups):
            inject[seg * SUB : (seg + 1) * SUB, k * LANES : (k + 1) * LANES] = inject_tiles[seg * groups + k]
    for k in range(groups):
        cols = slice(k * LANES, (k + 1) * LANES)
        inject_t[cols, :] = inject[:, cols].T
    transpose_matrices(mats, mats_t, groups)
    copy_seen.wait()
    count = filtered.shape[0]
    run_chain(seen_now, mats, mats_t, inject, inject_t, start[...], filtered, out_t, False, 0, count)


def second_kernel(
    seen, earlier, mats, mats_t, inject, inject_t, block, error, prior, filtered, predicted, out_t, seen_now, sems, *, groups
):
    place = whereabouts()
    copy_seen = pltpu.make_async_copy(seen, seen_now, sems.at[0])
    copy_seen.start()
    done = earlier.shape[0]
    filtered[:done, :] = earlier[...]
    start = earlier[done - 1 : done, :]
    copy_seen.wait()
    count = filtered.shape[0] - done
    run_chain(seen_now, mats, mats_t, inject, inject_t, start, filtered, out_t, False, done, count)
    send_block(place, filtered, block, sems.at[1])
    predict(filtered, mats_t, predicted, groups)
    row = lax.broadcasted_iota(jnp.int32, (filtered.shape[0], LANES), 0)
    for k in range(groups):
        cols = slice(k * LANES, (k + 1) * LANES)
        shifted = jnp.where(row == 0, 0.0, pltpu.roll(predicted[:, cols], 1, 0))
        prior[:, cols] = shifted
        error[:, cols] = filtered[:, cols] - shifted
    pltpu.make_async_copy(filtered.at[: block.shape[0], : block.shape[1]], block, sems.at[1]).wait()


def backward_kernel(seen, error, prior, *refs, groups):
    own, par = refs[:SIDE], refs[SIDE : 2 * SIDE]
    block, smoothed, mats, mats_t, inject_t, out_t, seen_now, sems = refs[2 * SIDE :]
    blocks = 2 * groups
    place = whereabouts()
    copy_seen = pltpu.make_async_copy(seen, seen_now, sems.at[0])
    copy_seen.start()
    load_matrices(place, own, par, mats, blocks)
    for k in range(groups):
        cols = slice(k * LANES, (k + 1) * LANES)
        inject_t[cols, :] = error[:, cols].T
    transpose_matrices(mats, mats_t, groups)
    copy_seen.wait()
    start = jnp.zeros((1, smoothed.shape[1]), jnp.float32)
    run_chain(seen_now, mats, mats_t, error, inject_t, start, smoothed, out_t, True, 0, smoothed.shape[0])
    smoothed[...] += prior[...]
    send_block(place, smoothed, block, sems.at[1])
    pltpu.make_async_copy(smoothed.at[: block.shape[0], : block.shape[1]], block, sems.at[1]).wait()


def shards(observations, observed, start_mean, transition, closed_loop, obs_gain, smooth_observed, smooth_missing):
    seg_steps, dim = observations.shape
    groups = dim // LANES
    steps = seg_steps * lax.axis_size("tm")
    c = lax.axis_index("rows") % CORES
    is_zero = c == 0

    fwd_0, fwd_1 = tiles(transition), tiles(closed_loop)
    bwd_0, bwd_1 = tiles(smooth_missing), tiles(smooth_observed)
    set_0 = jnp.stack([fwd_0, bwd_0])
    set_1 = jnp.stack([fwd_1, bwd_1])
    mine = jnp.where(is_zero, set_0, set_1)
    other = swap_cores(jnp.where(is_zero, set_1, set_0))
    unit = jnp.where(is_zero, jnp.concatenate([mine, other], 1), jnp.concatenate([other, mine], 1))

    gain_rows = lax.dynamic_slice_in_dim(obs_gain, c * (dim // 2), dim // 2, 0)
    seen_float = observed.astype(jnp.float32)
    inject = (
        lax.dot_general(observations, gain_rows, (((1,), (1,)), ((), ())), precision=lax.Precision.HIGHEST)
        * seen_float[:, None]
    )
    level = [unit]
    for k in range(1, SIDE):
        level.append(along_z(unit, k))
    inject = lax.optimization_barrier(inject)
    seen_tile = jnp.broadcast_to(seen_float[:, None], (seg_steps, LANES))[None]
    packed = jnp.concatenate([u[0] for u in level] + [tiles(inject), seen_tile] + [u[1] for u in level], 0)
    cut = SIDE * 2 * groups + groups // 2 + 1

    packs = [packed] + [across(packed, k, 0) for k in range(1, SIDE)]
    fwd = jnp.stack([p[:cut] for p in packs])
    bwd = jnp.stack([p[cut:] for p in packs])
    fwd_own = [fwd] + [across(fwd, k, 1) for k in range(1, SIDE)]
    fwd_par = [swap_cores(v) for v in fwd_own]
    bwd_own = [bwd] + [across(bwd, k, 1) for k in range(1, SIDE)]
    vmem = pl.BlockSpec(memory_space=pltpu.VMEM)
    any_space = pl.BlockSpec(memory_space=pl.ANY)

    def shape(*sizes):
        return jax.ShapeDtypeStruct(sizes, jnp.float32)

    segs = steps // SUB
    first_steps = steps * FIRST_STEPS // LANES // SUB * SUB
    mats_shape = (2, dim // SUB * groups, SUB, LANES)
    mats = pltpu.VMEM(mats_shape, jnp.float32)
    wide = pltpu.VMEM((steps, dim), jnp.float32)
    tall = pltpu.VMEM((dim, steps), jnp.float32)
    seen_now = pltpu.SMEM((segs, LANES), jnp.float32)
    out_block = shape(seg_steps, LANES)
    earlier, fwd_mats, fwd_mats_t, inject, inject_t, seen = pl.pallas_call(
        partial(first_kernel, groups=groups),
        out_shape=(
            shape(first_steps, dim),
            shape(*mats_shape),
            shape(*mats_shape),
            shape(steps, dim),
            shape(dim, steps),
            shape(segs, LANES),
        ),
        in_specs=[vmem] * (1 + 2 * SIDE),
        out_specs=(vmem,) * 6,
        scratch_shapes=[pltpu.VMEM((segs * groups, SUB, LANES), jnp.float32), tall, seen_now, pltpu.SemaphoreType.DMA((1,))],
        compiler_params=pltpu.CompilerParams(vmem_limit_bytes=FIRST_BYTES),
        name="forward_first",
    )(start_mean.reshape(1, dim), *fwd_own, *fwd_par)

    *moved, earlier = lax.optimization_barrier((*bwd_own[1:], earlier))
    bwd_own = bwd_own[:1] + moved
    bwd_par = [swap_cores(v) for v in bwd_own]
    filtered, error, prior = pl.pallas_call(
        partial(second_kernel, groups=groups),
        out_shape=(out_block, shape(steps, dim), shape(steps, dim)),
        in_specs=[vmem] * 6,
        out_specs=(any_space, vmem, vmem),
        scratch_shapes=[wide, wide, tall, seen_now, pltpu.SemaphoreType.DMA((2,))],
        compiler_params=pltpu.CompilerParams(vmem_limit_bytes=FIRST_BYTES),
        name="forward_second",
    )(seen, earlier, fwd_mats, fwd_mats_t, inject, inject_t)

    smoothed = pl.pallas_call(
        partial(backward_kernel, groups=groups),
        out_shape=out_block,
        in_specs=[vmem] * (3 + 2 * SIDE),
        out_specs=any_space,
        scratch_shapes=[wide, mats, mats, tall, tall, seen_now, pltpu.SemaphoreType.DMA((2,))],
        compiler_params=pltpu.CompilerParams(vmem_limit_bytes=VMEM_BYTES),
        name="backward_chain",
    )(seen, error, prior, *bwd_own, *bwd_par)
    return filtered, smoothed


def solution(mesh):
    return jax.shard_map(
        shards,
        mesh=mesh,
        in_specs=(
            P("tm", None),
            P("tm"),
            P(),
            P(("tm", "rows"), None),
            P(("tm", "rows"), None),
            P(),
            P(("tm", "rows"), None),
            P(("tm", "rows"), None),
        ),
        out_specs=(P("tm", "rows"), P("tm", "rows")),
        check_vma=False,
    )
```

```python
from functools import partial

import jax
import jax.numpy as jnp
from jax import lax
from jax.experimental import pallas as pl
from jax.experimental.pallas import tpu as pltpu
from jax.sharding import PartitionSpec as P


ALL = ("tm", "rows")
SIDE = 4
CORES = 2
LANES = 128
SUB = 8
UNROLL = 128
FIRST_STEPS = 80
VMEM_BYTES = 28 << 20
FIRST_BYTES = 8 << 20


def device_id(y, x, z, c):
    return ((y % SIDE * SIDE + x % SIDE) * SIDE + z % SIDE) * CORES + c


def coords():
    return [(y, x, z, c) for y in range(SIDE) for x in range(SIDE) for z in range(SIDE) for c in range(CORES)]


def swap_cores(value):
    return lax.ppermute(value, ALL, [(device_id(y, x, z, c), device_id(y, x, z, 1 - c)) for y, x, z, c in coords()])


def along_z(value, k):
    return lax.ppermute(value, ALL, [(device_id(y, x, z, c), device_id(y, x, z + k, c)) for y, x, z, c in coords()])


def across(value, k, phase):
    pairs = []
    for y, x, z, c in coords():
        dx = k if (c == 0) == (phase == 0) else 0
        dy = k - dx
        pairs.append((device_id(y, x, z, c), device_id(y + dy, x + dx, z, c)))
    return lax.ppermute(value, ALL, pairs)


def tiles(rows):
    r, width = rows.shape
    n = width // LANES
    return rows.reshape(r // SUB, SUB, n, LANES).transpose(0, 2, 1, 3).reshape(r // SUB * n, SUB, LANES)


def wrap(position):
    return jnp.bitwise_and(position, SIDE - 1)


def whereabouts():
    tm = lax.axis_index("tm")
    rows = lax.axis_index("rows")
    return tm // SIDE, tm % SIDE, rows // CORES, rows % CORES


def load_matrices(place, own, par, mats, blocks):
    y, x, z, c = place

    def move(i, carry):
        k2 = jnp.right_shift(i, SIDE.bit_length() - 1)
        kz = wrap(i)
        pz = wrap(z - kz)
        for k3 in range(SIDE):
            for mine in (True, False):
                q = c if mine else 1 - c
                dy = jnp.where(q == 0, k3, k2)
                dx = jnp.where(q == 0, k2, k3)
                chip = (wrap(y - dy) * SIDE + wrap(x - dx)) * SIDE + pz
                src = (own if mine else par)[k3]
                there = pl.ds(pl.multiple_of(chip * blocks, blocks), blocks)
                mats[q, there] = src[k2, pl.ds(pl.multiple_of(kz * blocks, blocks), blocks)]
        return carry

    lax.fori_loop(0, SIDE * SIDE, move, 0)


def load_inject(place, own, par, inject, first, count):
    y, x, _, c = place

    def move(k2, carry):
        for k3 in range(SIDE):
            for mine in (True, False):
                q = c if mine else 1 - c
                dy = jnp.where(q == 0, k3, k2)
                dx = jnp.where(q == 0, k2, k3)
                seg = wrap(y - dy) * SIDE + wrap(x - dx)
                src = (own if mine else par)[k3]
                inject[pl.ds(seg * 2 * count + q * count, count)] = src[k2, first : first + count]
        return carry

    lax.fori_loop(0, SIDE, move, 0)


def load_seen(place, own, seen, first):
    y, x, _, c = place
    lane = lax.broadcasted_iota(jnp.int32, (SUB, LANES), 1)
    sub = lax.broadcasted_iota(jnp.int32, (SUB, LANES), 0)
    for k3 in range(SIDE):
        for k2 in range(SIDE):
            dy = jnp.where(c == 0, k3, k2)
            dx = jnp.where(c == 0, k2, k3)
            seg = wrap(y - dy) * SIDE + wrap(x - dx)
            flags = jnp.where(lane == sub, own[k3][k2, first], 0.0)
            seen[pl.ds(seg, 1), :] = jnp.sum(flags, 0, keepdims=True)


def transpose_matrices(mats, mats_t, groups):
    def block_row(b, carry):
        for s in range(2):
            for k in range(groups):
                rows = [mats[s, (b * 16 + r) * groups + k] for r in range(16)]
                flipped = jnp.concatenate(rows, 0).T
                for r in range(16):
                    mats_t[s, (k * 16 + r) * groups + b] = flipped[r * SUB : (r + 1) * SUB]
        return carry

    lax.fori_loop(0, groups, block_row, 0)


def run_chain(seen, mats, mats_t, inject, inject_t, start, out, out_t, reverse, begin, count):
    steps, dim = inject.shape
    groups = dim // LANES
    row_blocks = dim // SUB
    lane = lax.broadcasted_iota(jnp.int32, (SUB, LANES), 1)

    def pick(t):
        return (seen[t // SUB, t % SUB] > 0.5).astype(jnp.int32)

    def pair(p, row):
        first = steps - 1 - begin - 2 * p if reverse else begin + 2 * p
        second = first - 1 if reverse else first + 1
        s0, s1 = pick(first), pick(second)
        here = lane == first
        state = [jnp.broadcast_to(row[:, k * LANES : (k + 1) * LANES], (SUB, LANES)) for k in range(groups)]

        def rows(j, sums):
            r = pl.multiple_of(j * SUB, SUB)
            a = mats[s0, pl.ds(j * groups, groups)]
            prods = [a[k] * state[k] for k in range(groups)]
            while len(prods) > 1:
                prods = [prods[i] + prods[i + 1] for i in range(0, len(prods), 2)]
            total = prods[0] + jnp.where(here, inject_t[pl.ds(r, SUB), :], 0.0)
            col = jnp.broadcast_to(jnp.sum(total, 1, keepdims=True), (SUB, LANES))
            pltpu.store(out_t.at[pl.ds(r, SUB), :], col, mask=here)
            b = mats_t[s1, pl.ds(j * groups, groups)]
            return tuple(sums[k] + b[k] * col for k in range(groups))

        zero = tuple(jnp.zeros((SUB, LANES), jnp.float32) for _ in range(groups))
        sums = lax.fori_loop(0, row_blocks, rows, zero, unroll=UNROLL)
        row = jnp.concatenate([jnp.sum(v, 0, keepdims=True) for v in sums], 1) + inject[pl.ds(second, 1), :]
        out[pl.ds(second, 1), :] = row
        return row

    lax.fori_loop(0, count // 2, pair, start)
    low = steps - begin - count if reverse else begin
    odd = lax.broadcasted_iota(jnp.int32, (count, LANES), 0) % 2
    from_t = odd == (1 if reverse else 0)
    for k in range(groups):
        cols = slice(k * LANES, (k + 1) * LANES)
        flipped = out_t[cols, :].T[low : low + count]
        out[low : low + count, cols] = jnp.where(from_t, flipped, out[low : low + count, cols])


def split(value):
    high = value.astype(jnp.bfloat16)
    return high, (value - high.astype(jnp.float32)).astype(jnp.bfloat16)


def predict(states, mats_t, out, groups):
    high, low = split(states[...])
    dot = partial(jnp.dot, preferred_element_type=jnp.float32)
    width = 2
    for b in range(0, groups, width):
        weights = jnp.concatenate(
            [
                jnp.concatenate([mats_t[0, j * groups + b + i] for j in range(groups * 16)], 0)
                for i in range(width)
            ],
            1,
        )
        w_high, w_low = split(weights)
        out[:, b * LANES : (b + width) * LANES] = dot(high, w_high) + (dot(low, w_high) + dot(high, w_low))


def send_block(place, value, block, sem):
    y, x, z, c = place
    seg_steps, width = block.shape
    corner = pl.ds((y * SIDE + x) * seg_steps, seg_steps), pl.ds((z * CORES + c) * width, width)
    pltpu.make_async_copy(value.at[corner], block, sem).start()


def first_kernel(start, *refs, groups):
    own, par = refs[:SIDE], refs[SIDE : 2 * SIDE]
    filtered, mats, mats_t, inject, inject_t, seen, inject_tiles, out_t, seen_now, sem = refs[2 * SIDE :]
    blocks = 2 * groups
    half = groups // 2
    place = whereabouts()
    load_seen(place, own, seen, SIDE * blocks + half)
    copy_seen = pltpu.make_async_copy(seen, seen_now, sem.at[0])
    copy_seen.start()
    load_matrices(place, own, par, mats, blocks)
    load_inject(place, own, par, inject_tiles, SIDE * blocks, half)
    for seg in range(inject_tiles.shape[0] // groups):
        for k in range(groups):
            inject[seg * SUB : (seg + 1) * SUB, k * LANES : (k + 1) * LANES] = inject_tiles[seg * groups + k]
    for k in range(groups):
        cols = slice(k * LANES, (k + 1) * LANES)
        inject_t[cols, :] = inject[:, cols].T
    transpose_matrices(mats, mats_t, groups)
    copy_seen.wait()
    count = filtered.shape[0]
    run_chain(seen_now, mats, mats_t, inject, inject_t, start[...], filtered, out_t, False, 0, count)


def second_kernel(
    seen, earlier, mats, mats_t, inject, inject_t, block, error, prior, filtered, predicted, out_t, seen_now, sems, *, groups
):
    place = whereabouts()
    copy_seen = pltpu.make_async_copy(seen, seen_now, sems.at[0])
    copy_seen.start()
    done = earlier.shape[0]
    filtered[:done, :] = earlier[...]
    start = earlier[done - 1 : done, :]
    copy_seen.wait()
    count = filtered.shape[0] - done
    run_chain(seen_now, mats, mats_t, inject, inject_t, start, filtered, out_t, False, done, count)
    send_block(place, filtered, block, sems.at[1])
    predict(filtered, mats_t, predicted, groups)
    row = lax.broadcasted_iota(jnp.int32, (filtered.shape[0], LANES), 0)
    for k in range(groups):
        cols = slice(k * LANES, (k + 1) * LANES)
        shifted = jnp.where(row == 0, 0.0, pltpu.roll(predicted[:, cols], 1, 0))
        prior[:, cols] = shifted
        error[:, cols] = filtered[:, cols] - shifted
    pltpu.make_async_copy(filtered.at[: block.shape[0], : block.shape[1]], block, sems.at[1]).wait()


def backward_kernel(seen, error, prior, *refs, groups):
    own, par = refs[:SIDE], refs[SIDE : 2 * SIDE]
    block, smoothed, mats, mats_t, inject_t, out_t, seen_now, sems = refs[2 * SIDE :]
    blocks = 2 * groups
    place = whereabouts()
    copy_seen = pltpu.make_async_copy(seen, seen_now, sems.at[0])
    copy_seen.start()
    load_matrices(place, own, par, mats, blocks)
    for k in range(groups):
        cols = slice(k * LANES, (k + 1) * LANES)
        inject_t[cols, :] = error[:, cols].T
    transpose_matrices(mats, mats_t, groups)
    copy_seen.wait()
    start = jnp.zeros((1, smoothed.shape[1]), jnp.float32)
    run_chain(seen_now, mats, mats_t, error, inject_t, start, smoothed, out_t, True, 0, smoothed.shape[0])
    smoothed[...] += prior[...]
    send_block(place, smoothed, block, sems.at[1])
    pltpu.make_async_copy(smoothed.at[: block.shape[0], : block.shape[1]], block, sems.at[1]).wait()


def shards(observations, observed, start_mean, transition, closed_loop, obs_gain, smooth_observed, smooth_missing):
    seg_steps, dim = observations.shape
    groups = dim // LANES
    steps = seg_steps * lax.axis_size("tm")
    c = lax.axis_index("rows") % CORES
    is_zero = c == 0

    fwd_0, fwd_1 = tiles(transition), tiles(closed_loop)
    bwd_0, bwd_1 = tiles(smooth_missing), tiles(smooth_observed)
    set_0 = jnp.stack([fwd_0, bwd_0])
    set_1 = jnp.stack([fwd_1, bwd_1])
    mine = jnp.where(is_zero, set_0, set_1)
    other = swap_cores(jnp.where(is_zero, set_1, set_0))
    unit = jnp.where(is_zero, jnp.concatenate([mine, other], 1), jnp.concatenate([other, mine], 1))

    gain_rows = lax.dynamic_slice_in_dim(obs_gain, c * (dim // 2), dim // 2, 0)
    seen_float = observed.astype(jnp.float32)
    inject = (
        lax.dot_general(observations, gain_rows, (((1,), (1,)), ((), ())), precision=lax.Precision.HIGHEST)
        * seen_float[:, None]
    )
    level = [unit]
    for k in range(1, SIDE):
        level.append(along_z(unit, k))
    inject = lax.optimization_barrier(inject)
    seen_tile = jnp.broadcast_to(seen_float[:, None], (seg_steps, LANES))[None]
    packed = jnp.concatenate([u[0] for u in level] + [tiles(inject), seen_tile] + [u[1] for u in level], 0)
    cut = SIDE * 2 * groups + groups // 2 + 1

    packs = [packed] + [across(packed, k, 0) for k in range(1, SIDE)]
    fwd = jnp.stack([p[:cut] for p in packs])
    bwd = jnp.stack([p[cut:] for p in packs])
    fwd_own = [fwd] + [across(fwd, k, 1) for k in range(1, SIDE)]
    fwd_par = [swap_cores(v) for v in fwd_own]
    bwd_own = [bwd] + [across(bwd, k, 1) for k in range(1, SIDE)]
    vmem = pl.BlockSpec(memory_space=pltpu.VMEM)
    any_space = pl.BlockSpec(memory_space=pl.ANY)

    def shape(*sizes):
        return jax.ShapeDtypeStruct(sizes, jnp.float32)

    segs = steps // SUB
    first_steps = steps * FIRST_STEPS // LANES // SUB * SUB
    mats_shape = (2, dim // SUB * groups, SUB, LANES)
    mats = pltpu.VMEM(mats_shape, jnp.float32)
    wide = pltpu.VMEM((steps, dim), jnp.float32)
    tall = pltpu.VMEM((dim, steps), jnp.float32)
    seen_now = pltpu.SMEM((segs, LANES), jnp.float32)
    out_block = shape(seg_steps, LANES)
    earlier, fwd_mats, fwd_mats_t, inject, inject_t, seen = pl.pallas_call(
        partial(first_kernel, groups=groups),
        out_shape=(
            shape(first_steps, dim),
            shape(*mats_shape),
            shape(*mats_shape),
            shape(steps, dim),
            shape(dim, steps),
            shape(segs, LANES),
        ),
        in_specs=[vmem] * (1 + 2 * SIDE),
        out_specs=(vmem,) * 6,
        scratch_shapes=[pltpu.VMEM((segs * groups, SUB, LANES), jnp.float32), tall, seen_now, pltpu.SemaphoreType.DMA((1,))],
        compiler_params=pltpu.CompilerParams(vmem_limit_bytes=FIRST_BYTES),
        name="forward_first",
    )(start_mean.reshape(1, dim), *fwd_own, *fwd_par)

    *moved, earlier = lax.optimization_barrier((*bwd_own[1:], earlier))
    bwd_own = bwd_own[:1] + moved
    bwd_par = [swap_cores(v) for v in bwd_own]
    filtered, error, prior = pl.pallas_call(
        partial(second_kernel, groups=groups),
        out_shape=(out_block, shape(steps, dim), shape(steps, dim)),
        in_specs=[vmem] * 6,
        out_specs=(any_space, vmem, vmem),
        scratch_shapes=[wide, wide, tall, seen_now, pltpu.SemaphoreType.DMA((2,))],
        compiler_params=pltpu.CompilerParams(vmem_limit_bytes=FIRST_BYTES),
        name="forward_second",
    )(seen, earlier, fwd_mats, fwd_mats_t, inject, inject_t)

    smoothed = pl.pallas_call(
        partial(backward_kernel, groups=groups),
        out_shape=out_block,
        in_specs=[vmem] * (3 + 2 * SIDE),
        out_specs=any_space,
        scratch_shapes=[wide, mats, mats, tall, tall, seen_now, pltpu.SemaphoreType.DMA((2,))],
        compiler_params=pltpu.CompilerParams(vmem_limit_bytes=VMEM_BYTES),
        name="backward_chain",
    )(seen, error, prior, *bwd_own, *bwd_par)
    return filtered, smoothed


def solution(mesh):
    return jax.shard_map(
        shards,
        mesh=mesh,
        in_specs=(
            P("tm", None),
            P("tm"),
            P(),
            P(("tm", "rows"), None),
            P(("tm", "rows"), None),
            P(),
            P(("tm", "rows"), None),
            P(("tm", "rows"), None),
        ),
        out_specs=(P("tm", "rows"), P("tm", "rows")),
        check_vma=False,
    )
```

```python
from functools import partial

import jax
import jax.numpy as jnp
from jax import lax
from jax.experimental import pallas as pl
from jax.experimental.pallas import tpu as pltpu
from jax.sharding import PartitionSpec as P


ALL = ("tm", "rows")
SIDE = 4
CORES = 2
LANES = 128
SUB = 8
UNROLL = 128
FIRST_STEPS = 80
VMEM_BYTES = 28 << 20
FIRST_BYTES = 8 << 20


def device_id(y, x, z, c):
    return ((y % SIDE * SIDE + x % SIDE) * SIDE + z % SIDE) * CORES + c


def coords():
    return [(y, x, z, c) for y in range(SIDE) for x in range(SIDE) for z in range(SIDE) for c in range(CORES)]


def swap_cores(value):
    return lax.ppermute(value, ALL, [(device_id(y, x, z, c), device_id(y, x, z, 1 - c)) for y, x, z, c in coords()])


def along_z(value, k):
    return lax.ppermute(value, ALL, [(device_id(y, x, z, c), device_id(y, x, z + k, c)) for y, x, z, c in coords()])


def across(value, k, phase):
    pairs = []
    for y, x, z, c in coords():
        dx = k if (c == 0) == (phase == 0) else 0
        dy = k - dx
        pairs.append((device_id(y, x, z, c), device_id(y + dy, x + dx, z, c)))
    return lax.ppermute(value, ALL, pairs)


def tiles(rows):
    r, width = rows.shape
    n = width // LANES
    return rows.reshape(r // SUB, SUB, n, LANES).transpose(0, 2, 1, 3).reshape(r // SUB * n, SUB, LANES)


def wrap(position):
    return jnp.bitwise_and(position, SIDE - 1)


def whereabouts():
    tm = lax.axis_index("tm")
    rows = lax.axis_index("rows")
    return tm // SIDE, tm % SIDE, rows // CORES, rows % CORES


def load_matrices(place, own, par, mats, blocks):
    y, x, z, c = place

    def move(i, carry):
        k2 = jnp.right_shift(i, SIDE.bit_length() - 1)
        kz = wrap(i)
        pz = wrap(z - kz)
        for k3 in range(SIDE):
            for mine in (True, False):
                q = c if mine else 1 - c
                dy = jnp.where(q == 0, k3, k2)
                dx = jnp.where(q == 0, k2, k3)
                chip = (wrap(y - dy) * SIDE + wrap(x - dx)) * SIDE + pz
                src = (own if mine else par)[k3]
                there = pl.ds(pl.multiple_of(chip * blocks, blocks), blocks)
                mats[q, there] = src[k2, pl.ds(pl.multiple_of(kz * blocks, blocks), blocks)]
        return carry

    lax.fori_loop(0, SIDE * SIDE, move, 0)


def load_inject(place, own, par, inject, first, count):
    y, x, _, c = place

    def move(k2, carry):
        for k3 in range(SIDE):
            for mine in (True, False):
                q = c if mine else 1 - c
                dy = jnp.where(q == 0, k3, k2)
                dx = jnp.where(q == 0, k2, k3)
                seg = wrap(y - dy) * SIDE + wrap(x - dx)
                src = (own if mine else par)[k3]
                inject[pl.ds(seg * 2 * count + q * count, count)] = src[k2, first : first + count]
        return carry

    lax.fori_loop(0, SIDE, move, 0)


def load_seen(place, own, seen, first):
    y, x, _, c = place
    lane = lax.broadcasted_iota(jnp.int32, (SUB, LANES), 1)
    sub = lax.broadcasted_iota(jnp.int32, (SUB, LANES), 0)
    for k3 in range(SIDE):
        for k2 in range(SIDE):
            dy = jnp.where(c == 0, k3, k2)
            dx = jnp.where(c == 0, k2, k3)
            seg = wrap(y - dy) * SIDE + wrap(x - dx)
            flags = jnp.where(lane == sub, own[k3][k2, first], 0.0)
            seen[pl.ds(seg, 1), :] = jnp.sum(flags, 0, keepdims=True)


def transpose_matrices(mats, mats_t, groups):
    def block_row(b, carry):
        for s in range(2):
            for k in range(groups):
                rows = [mats[s, (b * 16 + r) * groups + k] for r in range(16)]
                flipped = jnp.concatenate(rows, 0).T
                for r in range(16):
                    mats_t[s, (k * 16 + r) * groups + b] = flipped[r * SUB : (r + 1) * SUB]
        return carry

    lax.fori_loop(0, groups, block_row, 0)


def run_chain(seen, mats, mats_t, inject, inject_t, start, out, out_t, reverse, begin, count):
    steps, dim = inject.shape
    groups = dim // LANES
    row_blocks = dim // SUB
    lane = lax.broadcasted_iota(jnp.int32, (SUB, LANES), 1)

    def pick(t):
        return (seen[jnp.right_shift(t, SUB.bit_length() - 1), jnp.bitwise_and(t, SUB - 1)] > 0.5).astype(jnp.int32)

    def times_of(p):
        first = steps - 1 - begin - 2 * p if reverse else begin + 2 * p
        return first, first - 1 if reverse else first + 1

    def picks(p):
        first, second = times_of(p)
        return pick(first), pick(second)

    def pair(p, carry):
        row, s0, s1 = carry
        first, second = times_of(p)
        upcoming = picks(jnp.minimum(p + 1, count // 2 - 1))
        here = lane == first
        state = [jnp.broadcast_to(row[:, k * LANES : (k + 1) * LANES], (SUB, LANES)) for k in range(groups)]

        def rows(j, sums):
            r = pl.multiple_of(j * SUB, SUB)
            a = mats[s0, pl.ds(j * groups, groups)]
            prods = [a[k] * state[k] for k in range(groups)]
            while len(prods) > 1:
                prods = [prods[i] + prods[i + 1] for i in range(0, len(prods), 2)]
            total = prods[0] + jnp.where(here, inject_t[pl.ds(r, SUB), :], 0.0)
            col = jnp.broadcast_to(jnp.sum(total, 1, keepdims=True), (SUB, LANES))
            pltpu.store(out_t.at[pl.ds(r, SUB), :], col, mask=here)
            b = mats_t[s1, pl.ds(j * groups, groups)]
            return tuple(sums[k] + b[k] * col for k in range(groups))

        zero = tuple(jnp.zeros((SUB, LANES), jnp.float32) for _ in range(groups))
        sums = lax.fori_loop(0, row_blocks, rows, zero, unroll=UNROLL)
        row = jnp.concatenate([jnp.sum(v, 0, keepdims=True) for v in sums], 1) + inject[pl.ds(second, 1), :]
        out[pl.ds(second, 1), :] = row
        return row, *upcoming

    lax.fori_loop(0, count // 2, pair, (start, *picks(0)))
    low = steps - begin - count if reverse else begin
    odd = lax.broadcasted_iota(jnp.int32, (count, LANES), 0) % 2
    from_t = odd == (1 if reverse else 0)
    for k in range(groups):
        cols = slice(k * LANES, (k + 1) * LANES)
        flipped = out_t[cols, :].T[low : low + count]
        out[low : low + count, cols] = jnp.where(from_t, flipped, out[low : low + count, cols])


def split(value):
    high = value.astype(jnp.bfloat16)
    return high, (value - high.astype(jnp.float32)).astype(jnp.bfloat16)


def predict(states, mats_t, out, groups):
    high, low = split(states[...])
    dot = partial(jnp.dot, preferred_element_type=jnp.float32)
    width = 2
    for b in range(0, groups, width):
        weights = jnp.concatenate(
            [
                jnp.concatenate([mats_t[0, j * groups + b + i] for j in range(groups * 16)], 0)
                for i in range(width)
            ],
            1,
        )
        w_high, w_low = split(weights)
        out[:, b * LANES : (b + width) * LANES] = dot(high, w_high) + (dot(low, w_high) + dot(high, w_low))


def send_block(place, value, block, sem):
    y, x, z, c = place
    seg_steps, width = block.shape
    corner = pl.ds((y * SIDE + x) * seg_steps, seg_steps), pl.ds((z * CORES + c) * width, width)
    pltpu.make_async_copy(value.at[corner], block, sem).start()


def first_kernel(start, *refs, groups):
    own, par = refs[:SIDE], refs[SIDE : 2 * SIDE]
    filtered, mats, mats_t, inject, inject_t, seen, inject_tiles, out_t, seen_now, sem = refs[2 * SIDE :]
    blocks = 2 * groups
    half = groups // 2
    place = whereabouts()
    load_seen(place, own, seen, SIDE * blocks + half)
    copy_seen = pltpu.make_async_copy(seen, seen_now, sem.at[0])
    copy_seen.start()
    load_matrices(place, own, par, mats, blocks)
    load_inject(place, own, par, inject_tiles, SIDE * blocks, half)
    for seg in range(inject_tiles.shape[0] // groups):
        for k in range(groups):
            inject[seg * SUB : (seg + 1) * SUB, k * LANES : (k + 1) * LANES] = inject_tiles[seg * groups + k]
    for k in range(groups):
        cols = slice(k * LANES, (k + 1) * LANES)
        inject_t[cols, :] = inject[:, cols].T
    transpose_matrices(mats, mats_t, groups)
    copy_seen.wait()
    count = filtered.shape[0]
    run_chain(seen_now, mats, mats_t, inject, inject_t, start[...], filtered, out_t, False, 0, count)


def second_kernel(
    seen, earlier, mats, mats_t, inject, inject_t, block, error, prior, filtered, predicted, out_t, seen_now, sems, *, groups
):
    place = whereabouts()
    copy_seen = pltpu.make_async_copy(seen, seen_now, sems.at[0])
    copy_seen.start()
    done = earlier.shape[0]
    filtered[:done, :] = earlier[...]
    start = earlier[done - 1 : done, :]
    copy_seen.wait()
    count = filtered.shape[0] - done
    run_chain(seen_now, mats, mats_t, inject, inject_t, start, filtered, out_t, False, done, count)
    send_block(place, filtered, block, sems.at[1])
    predict(filtered, mats_t, predicted, groups)
    row = lax.broadcasted_iota(jnp.int32, (filtered.shape[0], LANES), 0)
    for k in range(groups):
        cols = slice(k * LANES, (k + 1) * LANES)
        shifted = jnp.where(row == 0, 0.0, pltpu.roll(predicted[:, cols], 1, 0))
        prior[:, cols] = shifted
        error[:, cols] = filtered[:, cols] - shifted
    pltpu.make_async_copy(filtered.at[: block.shape[0], : block.shape[1]], block, sems.at[1]).wait()


def backward_kernel(seen, error, prior, *refs, groups):
    own, par = refs[:SIDE], refs[SIDE : 2 * SIDE]
    block, smoothed, mats, mats_t, inject_t, out_t, seen_now, sems = refs[2 * SIDE :]
    blocks = 2 * groups
    place = whereabouts()
    copy_seen = pltpu.make_async_copy(seen, seen_now, sems.at[0])
    copy_seen.start()
    load_matrices(place, own, par, mats, blocks)
    for k in range(groups):
        cols = slice(k * LANES, (k + 1) * LANES)
        inject_t[cols, :] = error[:, cols].T
    transpose_matrices(mats, mats_t, groups)
    copy_seen.wait()
    start = jnp.zeros((1, smoothed.shape[1]), jnp.float32)
    run_chain(seen_now, mats, mats_t, error, inject_t, start, smoothed, out_t, True, 0, smoothed.shape[0])
    smoothed[...] += prior[...]
    send_block(place, smoothed, block, sems.at[1])
    pltpu.make_async_copy(smoothed.at[: block.shape[0], : block.shape[1]], block, sems.at[1]).wait()


def shards(observations, observed, start_mean, transition, closed_loop, obs_gain, smooth_observed, smooth_missing):
    seg_steps, dim = observations.shape
    groups = dim // LANES
    steps = seg_steps * lax.axis_size("tm")
    c = lax.axis_index("rows") % CORES
    is_zero = c == 0

    fwd_0, fwd_1 = tiles(transition), tiles(closed_loop)
    bwd_0, bwd_1 = tiles(smooth_missing), tiles(smooth_observed)
    set_0 = jnp.stack([fwd_0, bwd_0])
    set_1 = jnp.stack([fwd_1, bwd_1])
    mine = jnp.where(is_zero, set_0, set_1)
    other = swap_cores(jnp.where(is_zero, set_1, set_0))
    unit = jnp.where(is_zero, jnp.concatenate([mine, other], 1), jnp.concatenate([other, mine], 1))

    gain_rows = lax.dynamic_slice_in_dim(obs_gain, c * (dim // 2), dim // 2, 0)
    seen_float = observed.astype(jnp.float32)
    inject = (
        lax.dot_general(observations, gain_rows, (((1,), (1,)), ((), ())), precision=lax.Precision.HIGHEST)
        * seen_float[:, None]
    )
    level = [unit]
    for k in range(1, SIDE):
        level.append(along_z(unit, k))
    inject = lax.optimization_barrier(inject)
    seen_tile = jnp.broadcast_to(seen_float[:, None], (seg_steps, LANES))[None]
    packed = jnp.concatenate([u[0] for u in level] + [tiles(inject), seen_tile] + [u[1] for u in level], 0)
    cut = SIDE * 2 * groups + groups // 2 + 1

    packs = [packed] + [across(packed, k, 0) for k in range(1, SIDE)]
    fwd = jnp.stack([p[:cut] for p in packs])
    bwd = jnp.stack([p[cut:] for p in packs])
    fwd_own = [fwd] + [across(fwd, k, 1) for k in range(1, SIDE)]
    fwd_par = [swap_cores(v) for v in fwd_own]
    bwd_own = [bwd] + [across(bwd, k, 1) for k in range(1, SIDE)]
    vmem = pl.BlockSpec(memory_space=pltpu.VMEM)
    any_space = pl.BlockSpec(memory_space=pl.ANY)

    def shape(*sizes):
        return jax.ShapeDtypeStruct(sizes, jnp.float32)

    segs = steps // SUB
    first_steps = steps * FIRST_STEPS // LANES // SUB * SUB
    mats_shape = (2, dim // SUB * groups, SUB, LANES)
    mats = pltpu.VMEM(mats_shape, jnp.float32)
    wide = pltpu.VMEM((steps, dim), jnp.float32)
    tall = pltpu.VMEM((dim, steps), jnp.float32)
    seen_now = pltpu.SMEM((segs, LANES), jnp.float32)
    out_block = shape(seg_steps, LANES)
    earlier, fwd_mats, fwd_mats_t, inject, inject_t, seen = pl.pallas_call(
        partial(first_kernel, groups=groups),
        out_shape=(
            shape(first_steps, dim),
            shape(*mats_shape),
            shape(*mats_shape),
            shape(steps, dim),
            shape(dim, steps),
            shape(segs, LANES),
        ),
        in_specs=[vmem] * (1 + 2 * SIDE),
        out_specs=(vmem,) * 6,
        scratch_shapes=[pltpu.VMEM((segs * groups, SUB, LANES), jnp.float32), tall, seen_now, pltpu.SemaphoreType.DMA((1,))],
        compiler_params=pltpu.CompilerParams(vmem_limit_bytes=FIRST_BYTES),
        name="forward_first",
    )(start_mean.reshape(1, dim), *fwd_own, *fwd_par)

    *moved, earlier = lax.optimization_barrier((*bwd_own[1:], earlier))
    bwd_own = bwd_own[:1] + moved
    bwd_par = [swap_cores(v) for v in bwd_own]
    filtered, error, prior = pl.pallas_call(
        partial(second_kernel, groups=groups),
        out_shape=(out_block, shape(steps, dim), shape(steps, dim)),
        in_specs=[vmem] * 6,
        out_specs=(any_space, vmem, vmem),
        scratch_shapes=[wide, wide, tall, seen_now, pltpu.SemaphoreType.DMA((2,))],
        compiler_params=pltpu.CompilerParams(vmem_limit_bytes=FIRST_BYTES),
        name="forward_second",
    )(seen, earlier, fwd_mats, fwd_mats_t, inject, inject_t)

    smoothed = pl.pallas_call(
        partial(backward_kernel, groups=groups),
        out_shape=out_block,
        in_specs=[vmem] * (3 + 2 * SIDE),
        out_specs=any_space,
        scratch_shapes=[wide, mats, mats, tall, tall, seen_now, pltpu.SemaphoreType.DMA((2,))],
        compiler_params=pltpu.CompilerParams(vmem_limit_bytes=VMEM_BYTES),
        name="backward_chain",
    )(seen, error, prior, *bwd_own, *bwd_par)
    return filtered, smoothed


def solution(mesh):
    return jax.shard_map(
        shards,
        mesh=mesh,
        in_specs=(
            P("tm", None),
            P("tm"),
            P(),
            P(("tm", "rows"), None),
            P(("tm", "rows"), None),
            P(),
            P(("tm", "rows"), None),
            P(("tm", "rows"), None),
        ),
        out_specs=(P("tm", "rows"), P("tm", "rows")),
        check_vma=False,
    )
```
